256 devices in a mesh: layer: 8 (over z_hi, y), ex: 32 (over z_lo, x, core).
Axes of the slice: x: 4, y: 4, z: 8 (z_hi: 2, z_lo: 4; z = z_hi * 4 + z_lo), core: 2. Of those that a mesh axis runs over, the one named last changes fastest.
Arguments:
- train_ids: int32 [64, 64], P('ex'), may hold values from 0 to 128001, as said below
- query_ids: int32 [64, 16], P('ex'), may hold values from 0 to 128001, as said below
- train_inputs: bfloat16 [8, 4096, 8192], P('layer', 'ex'), may hold values from -6 to 6
- train_grads: bfloat16 [8, 4096, 28672], P('layer', 'ex'), may hold values from -6 to 6
- query_inputs: bfloat16 [8, 1024, 8192], P('layer', 'ex'), may hold values from -6 to 6
- query_grads: bfloat16 [8, 1024, 28672], P('layer', 'ex'), may hold values from -6 to 6
- basis_in: bfloat16 [8, 8192, 256], P('layer', 'ex'), may hold values from -0.0625 to 0.0625
- basis_out: bfloat16 [8, 28672, 256], P('layer', 'ex'), may hold values from -0.03125 to 0.03125
- eigenvalues: float32 [8, 256, 256], P('layer'), may hold values from 0.1 to 10
Outputs:
- scores: float32 [64, 64], P('ex')
The draws below stay inside these ranges and needn't reach their ends.
Inputs may be any that keep to these rules, and one draw needn't show every extreme that they name: `train_ids`: each row holds the token ids of one training sequence from 0 to 127999 up to its live length, then the filler id 128001; live lengths run from 16 to 64. `query_ids`: each row holds the token ids of one query from 0 to 127999 up to its live length, then the filler id 128001; live lengths run from 4 to 16.
All inputs are finite; a program needn't handle non-finite values.
Results may differ from the reference program's by a relative error of at most 0.033.
Values may be sent and summed in bfloat16 or wider, within the bound.
No kernel may reach another device: no remote copies, remote signals or barrier semaphores. Data moves between devices by JAX's collectives and lax.ppermute only.
A program may use at most 128 MiB of HBM per device.

```python
import math
import jax
import jax.numpy as jnp
from jax import lax

D = 8192
F = 28672
KA = 256
KG = 256
SEQ = 64
QUERIES = 64
QLEN = 16
LAYERS = 8
EXAMPLES = 64
TOKENS = 4096
QTOKENS = 1024


def padded_ids(key, count, length):
    first, second = jax.random.split(key)
    tokens = jax.random.randint(first, (count, length), 0, 128000)
    live = jax.random.randint(second, (count, 1), length // 4, length + 1)
    position = jnp.arange(length)[None, :]
    return jnp.where(position < live, tokens, 128001).astype(jnp.int32)


def draw_train_ids(key, part):
    return padded_ids(jax.random.fold_in(key, 11), EXAMPLES, SEQ)


def draw_query_ids(key, part):
    return padded_ids(jax.random.fold_in(key, 23), QUERIES, QLEN)


def block_scale(stream_key, shape, shards, least, high):
    def one(axis_at, shards_of):
        draws = jax.random.uniform(jax.random.fold_in(jax.random.fold_in(stream_key, 6), axis_at), (shards_of,), jnp.float32, least / len(shards), high / len(shards))
        return jnp.repeat(jnp.exp(draws), shape[axis_at] // shards_of).reshape((-1,) + (1,) * (len(shape) - axis_at - 1))

    factor_of = one(*shards[0])
    for cut in shards[1:]:
        factor_of = factor_of * one(*cut)
    return factor_of


def scatter_about(rng, dims, scale, most, cuts=(), held_as=jnp.bfloat16):
    array = jax.random.normal(rng, dims, jnp.float32) * scale
    if len(cuts) > 0:
        array = block_scale(rng, dims, cuts, -0.22, 0.18) * array
    return jnp.clip(array, min=-most, max=most).astype(held_as)


def setup_inputs(seed: int = 0) -> dict:
    key_of = jax.random.split(jax.random.key(seed), 10)
    return {
        "train_ids": draw_train_ids(jax.random.fold_in(key_of[9], 71), 0),
        "query_ids": draw_query_ids(jax.random.fold_in(key_of[9], 71), 0),
        "train_inputs": scatter_about(key_of[2], (LAYERS, TOKENS, D), 1.0, 6.0, ((0, 8), (1, 32))),
        "train_grads": scatter_about(key_of[3], (LAYERS, TOKENS, F), 1.0, 6.0, ((0, 8), (1, 32))),
        "query_inputs": scatter_about(key_of[4], (LAYERS, QTOKENS, D), 1.0, 6.0, ((0, 8), (1, 32))),
        "query_grads": scatter_about(key_of[5], (LAYERS, QTOKENS, F), 1.0, 6.0, ((0, 8), (1, 32))),
        "basis_in": scatter_about(key_of[6], (LAYERS, D, KA), D ** -0.5, 0.0625, ((0, 8), (1, 32))),
        "basis_out": scatter_about(key_of[7], (LAYERS, F, KG), F ** -0.5, 0.03125, ((0, 8), (1, 32))),
        "eigenvalues": jnp.clip(jnp.exp(math.log(10.0) - 4.6051702 * jax.random.uniform(key_of[8], (LAYERS, KG, KA), jnp.float32) ** block_scale(key_of[8], (LAYERS, KG, KA), ((0, 8),), -0.2, 0.2)), 0.1, 10.0),
    }


filler_id = 128001
damping = 0.1

def rotate(inputs, grads, basis_in, basis_out, mask):
    rotated_in = jnp.dot(inputs, basis_in, preferred_element_type=jnp.float32).astype(jnp.bfloat16)
    rotated_out = jnp.dot(grads, basis_out, preferred_element_type=jnp.float32).astype(jnp.bfloat16)
    rotated_out = rotated_out * mask[:, None].astype(jnp.bfloat16)
    return (rotated_in, rotated_out)

def outer_sums(rotated_out, rotated_in, length):
    left = rotated_out.reshape(-1, length, rotated_out.shape[1])
    right = rotated_in.reshape(-1, length, rotated_in.shape[1])
    return jnp.einsum('stk,stl->skl', left, right, preferred_element_type=jnp.float32)

def reference(train_ids, query_ids, train_inputs, train_grads, query_inputs, query_grads, basis_in, basis_out, eigenvalues):
    train_mask = (train_ids != filler_id).astype(jnp.float32).reshape(-1)
    query_mask = (query_ids != filler_id).astype(jnp.float32).reshape(-1)

    def layer_scores(carry, index):
        rotated_in, rotated_out = rotate(train_inputs[index], train_grads[index], basis_in[index], basis_out[index], train_mask)
        query_in, query_out = rotate(query_inputs[index], query_grads[index], basis_in[index], basis_out[index], query_mask)
        example_grad = outer_sums(rotated_out, rotated_in, SEQ)
        query_grad = outer_sums(query_out, query_in, QLEN)
        precond = (query_grad / (eigenvalues[index] + damping)).astype(jnp.bfloat16)
        flat_examples = example_grad.reshape(EXAMPLES, KG * KA)
        flat_queries = precond.reshape(QUERIES, KG * KA).astype(jnp.float32)
        term = jnp.einsum('ek,qk->eq', flat_examples, flat_queries, precision=lax.Precision.HIGHEST)
        return (carry + term, None)
    start = jnp.zeros((EXAMPLES, QUERIES), jnp.float32)
    total, _ = lax.scan(layer_scores, start, jnp.arange(LAYERS, dtype=jnp.int32))
    return total / math.sqrt(KA * KG * SEQ * QLEN * LAYERS)
```

```python
import math

import jax
import jax.numpy as jnp
from jax import lax
from jax.experimental import pallas as pl
from jax.experimental.pallas import tpu as pltpu
from jax.sharding import PartitionSpec as P

filler_id = 128001
damping = 0.1
Z, X, C = 4, 4, 2
YS, ZH = 4, 2


def place(z, x, c):
    return (z * X + x) * C + c


def swaps(dz=0, dx=(0, 0), dc=0):
    return [
        (place(z, x, c), place(z ^ dz, x ^ dx[c], c ^ dc))
        for z in range(Z)
        for x in range(X)
        for c in range(C)
    ]


CORE = swaps(dc=1)
ALONG_A = swaps(dx=(1, 3))
ALONG_B = swaps(dx=(3, 1))


def gather_queries(mine):
    rows = [mine] + [lax.ppermute(mine, "ex", swaps(dz=s)) for s in (1, 2, 3)]
    column = jnp.concatenate(rows, axis=0)
    one = lax.ppermute(column, "ex", ALONG_A)
    two = lax.ppermute(column, "ex", ALONG_B)
    far = lax.ppermute(two, "ex", ALONG_A)
    held = [column, one, two, far]
    return held + [lax.ppermute(v, "ex", CORE) for v in held]


def weigh_kernel(rin_ref, rout_ref, eig_ref, w_ref):
    scale = 1.0 / (eig_ref[...] + damping)
    seqs = w_ref.shape[1] // eig_ref.shape[1]
    length = rin_ref.shape[0] // seqs
    width = eig_ref.shape[1]
    for e in range(seqs):
        rows = pl.ds(e * length, length)
        grad = lax.dot_general(
            rout_ref[rows, :], rin_ref[rows, :], (((0,), (0,)), ((), ())), preferred_element_type=jnp.float32
        )
        w_ref[:, e * width : (e + 1) * width] = (grad * scale).astype(w_ref.dtype)


def score_kernel(normal, query_len, where_ref, w_ref, *refs):
    pieces, out_ref = refs[:-1], refs[-1]
    z, x, c = where_ref[0], where_ref[1], where_ref[2]
    rows, both = pieces[0].shape
    width = both // 2
    seqs = w_ref.shape[1] // width
    queries = out_ref.shape[1]
    per = rows // Z
    row = lax.broadcasted_iota(jnp.int32, (rows, queries), 0)
    col = lax.broadcasted_iota(jnp.int32, (rows, queries), 1)
    totals = [jnp.zeros((1, queries), jnp.float32) for _ in range(seqs)]
    for i, piece in enumerate(pieces):
        lane = c if i < 4 else 1 - c
        dx = (0, 1 + 2 * lane, 3 - 2 * lane, 2)[i % 4]
        base = (x ^ dx) * C + lane
        source = (z ^ (row // per)) * (X * C) + base
        spot = source * (per // query_len) + (row % per) // query_len
        picked = spot == col
        asked_in = piece[:, :width].astype(jnp.float32)
        asked_out = piece[:, width:]
        turned = jnp.dot(asked_out, w_ref[...], preferred_element_type=jnp.float32)
        for e in range(seqs):
            term = jnp.sum(turned[:, e * width : (e + 1) * width] * asked_in, axis=1, keepdims=True)
            totals[e] = totals[e] + jnp.sum(jnp.where(picked, term, 0.0), axis=0, keepdims=True)
    out_ref[...] = jnp.concatenate(totals, axis=0) * normal


def over_layers(value):
    def swap(v, flip_y, flip_z):
        pairs = [(zh * YS + y, (zh ^ flip_z) * YS + (y ^ flip_y)) for zh in range(ZH) for y in range(YS)]
        return v + lax.ppermute(v, "layer", pairs)

    return swap(swap(swap(value, 1, 0), 3, 0), 0, 1)


def scores_of(rotated_in, rotated_out, asked, eigenvalues, query_len, normal):
    width_in, width_out = rotated_in.shape[1], rotated_out.shape[1]
    seqs = 2
    vmem = pl.BlockSpec(memory_space=pltpu.VMEM)
    w = pl.pallas_call(
        weigh_kernel,
        out_shape=jax.ShapeDtypeStruct((width_out, seqs * width_in), jnp.bfloat16),
        in_specs=[vmem] * 3,
        out_specs=vmem,
    )(rotated_in, rotated_out, eigenvalues)
    pieces = gather_queries(asked)
    me = lax.axis_index("ex")
    where = jnp.stack([me // (X * C), (me // C) % X, me % C]).astype(jnp.int32)
    queries = len(pieces) * pieces[0].shape[0] // query_len

    def kernel(*refs):
        score_kernel(normal, query_len, *refs)

    part = pl.pallas_call(
        kernel,
        out_shape=jax.ShapeDtypeStruct((seqs, queries), jnp.float32),
        in_specs=[pl.BlockSpec(memory_space=pltpu.SMEM)] + [vmem] * (1 + len(pieces)),
        out_specs=vmem,
    )(where, w, *pieces)
    return over_layers(part)


def local(
    train_ids,
    query_ids,
    train_inputs,
    train_grads,
    query_inputs,
    query_grads,
    basis_in,
    basis_out,
    eigenvalues,
):
    seq_len = train_ids.shape[1]
    query_len = query_ids.shape[1]
    width_in, width_out = basis_in.shape[2], basis_out.shape[2]
    train_mask = (train_ids != filler_id).astype(jnp.bfloat16).reshape(-1, 1)
    query_mask = (query_ids != filler_id).astype(jnp.bfloat16).reshape(-1, 1)
    piece = lax.all_gather(basis_in[0], "ex", axis=0, tiled=True)
    sum_in = jnp.dot(train_inputs[0], piece, preferred_element_type=jnp.float32)
    query_sum_in = jnp.dot(query_inputs[0], piece, preferred_element_type=jnp.float32)
    piece = lax.all_gather(basis_out[0], "ex", axis=0, tiled=True)
    sum_out = jnp.dot(train_grads[0], piece, preferred_element_type=jnp.float32)
    query_sum_out = jnp.dot(query_grads[0], piece, preferred_element_type=jnp.float32)
    rotated_in = sum_in.astype(jnp.bfloat16)
    rotated_out = sum_out.astype(jnp.bfloat16) * train_mask
    asked = jnp.concatenate(
        [query_sum_in.astype(jnp.bfloat16), query_sum_out.astype(jnp.bfloat16) * query_mask], axis=1
    )
    normal = 1.0 / math.sqrt(width_in * width_out * seq_len * query_len * lax.axis_size("layer"))
    return scores_of(rotated_in, rotated_out, asked, eigenvalues[0], query_len, normal)


def solution(mesh):
    assert mesh.shape["ex"] == Z * X * C and mesh.shape["layer"] == YS * ZH
    placed = (
        P("ex", None),
        P("ex", None),
        P("layer", "ex", None),
        P("layer", "ex", None),
        P("layer", "ex", None),
        P("layer", "ex", None),
        P("layer", "ex", None),
        P("layer", "ex", None),
        P("layer", None, None),
    )
    return jax.shard_map(
        local, mesh=mesh, in_specs=placed, out_specs=P("ex", None), check_vma=False
    )
```
